256 devices in a mesh: ctx: 2 (over core), head: 4 (over x), doc: 32 (over z, y).
Axes of the slice: x: 4, y: 4, z: 8, core: 2. Of those that a mesh axis runs over, the one named last changes fastest.
Arguments:
- queries: bfloat16 [32, 256, 8192], P('doc', 'ctx', 'head'), may hold values from -360 to 360
- keys: bfloat16 [32, 8192, 1024], P('doc', 'ctx', 'head'), may hold values from -6 to 6
- values: bfloat16 [32, 8192, 1024], P('doc', 'ctx', 'head'), may hold values from -6 to 6
- pattern: int32 [32, 2, 16], P('doc'), may hold values from 0 to 63, as said below
Outputs:
- attended: bfloat16 [32, 256, 8192], P('doc', 'ctx', 'head')
- gram: float32 [8192, 8192], P(('head', 'ctx'), 'doc')
The draws below stay inside these ranges and needn't reach their ends.
Inputs may be any that keep to these rules, and one draw needn't show every extreme that they name: Each row pattern[d, b, :] lists 16 different block numbers; no context shard (blocks s * 32 to (s + 1) * 32 - 1) holds more than 12 of one row's blocks, and in every draw some row has exactly 12 of its blocks in one shard.
All inputs are finite; a program needn't handle non-finite values.
Results may differ from the reference program's by a relative error of at most 0.015.
Values may be sent and summed in bfloat16 or wider, within the bound.
No kernel may reach another device: no remote copies, remote signals or barrier semaphores. Data moves between devices by JAX's collectives and lax.ppermute only.
A program may use at most 128 MiB of HBM per device.

```python
import jax
import jax.numpy as jnp
from jax import lax

D = 8192
QUERY_HEADS = 64
KEY_VALUE_HEADS = 8
HEAD_SIZE = 128
BLOCK_TOKENS = 128
TOPK_DEV = 8
NKB_DEV = 32
DOCUMENT_COUNT = 32
QB = 2
QLEN = 256
CACHE_BLOCKS = 64
CONTEXT_LENGTH = 8192
SELECTED_BLOCKS = 16
CAP = 12
N_CTX = 2


def draw_queries(key, part):
    base = jax.random.truncated_normal(key, -6.0, 6.0, (DOCUMENT_COUNT, QLEN, D), jnp.float32)
    return base.astype(jnp.bfloat16)


def draw_pattern(key, part):
    rows = DOCUMENT_COUNT * QB
    owners = N_CTX
    half = owners // 2
    pair_sum = 2 * TOPK_DEV
    first_key, owner_key, local_key, order_key, force_key = jax.random.split(jax.random.fold_in(key, 11), 5)
    first = jax.random.randint(first_key, (rows, half), pair_sum - CAP, CAP + 1)
    forced_row = jax.random.randint(force_key, (), 0, rows)
    forced = (jnp.arange(rows)[:, None] == forced_row) & (jnp.arange(half)[None, :] == 0)
    first = jnp.where(forced, CAP, first)
    paired = jnp.concatenate([first, pair_sum - first], axis=1)
    owner_order = jax.vmap(lambda k: jax.random.permutation(k, owners))(jax.random.split(owner_key, rows))
    counts = jnp.take_along_axis(paired, owner_order, axis=1)
    local = jax.vmap(lambda k: jax.random.permutation(k, NKB_DEV)[:CAP])(jax.random.split(local_key, rows * owners))
    local = local.reshape(rows, owners, CAP)
    slot = jnp.arange(CAP)[None, None, :]
    valid = (slot < counts[:, :, None]).reshape(rows, owners * CAP).astype(jnp.int32)
    blocks = (jnp.arange(owners)[None, :, None] * NKB_DEV + local).reshape(rows, owners * CAP)
    shuffle = jax.vmap(lambda k: jax.random.permutation(k, owners * CAP))(jax.random.split(order_key, rows))
    score = (1 - valid) * (owners * CAP) + shuffle
    order = jnp.argsort(score, axis=1)[:, :SELECTED_BLOCKS]
    return jnp.take_along_axis(blocks, order, axis=1).reshape(DOCUMENT_COUNT, QB, SELECTED_BLOCKS).astype(jnp.int32)


def level_of(key, extent, shards, smallest, largest):
    level = 1.0
    for axis_at, shards_of in shards:
        steps = jax.random.uniform(jax.random.fold_in(jax.random.fold_in(key, 6), axis_at), (shards_of,), jnp.float32, smallest / len(shards), largest / len(shards))
        level = level * jnp.repeat(jnp.exp(steps), extent[axis_at] // shards_of).reshape((-1,) + (1,) * (len(extent) - 1 - axis_at))
    return level


def noise(key, dims, scale, bound, pieces=(), dtype=jnp.bfloat16):
    drawn = jax.random.normal(key, dims, jnp.float32) * scale
    if len(pieces) > 0:
        drawn = level_of(key, dims, pieces, -0.22, 0.18) * drawn
    return jnp.clip(drawn, min=-bound, max=bound).astype(dtype)


def setup_inputs(seed: int = 0) -> dict:
    key_of = jax.random.split(jax.random.key(seed), 5)
    queries = draw_queries(jax.random.fold_in(key_of[4], 71), 0)
    keys = noise(key_of[1], (DOCUMENT_COUNT, CONTEXT_LENGTH, KEY_VALUE_HEADS * HEAD_SIZE), 1.0, 6.0, ((0, 32), (1, 2), (2, 4)))
    values = noise(key_of[2], (DOCUMENT_COUNT, CONTEXT_LENGTH, KEY_VALUE_HEADS * HEAD_SIZE), 1.0, 6.0, ((0, 32), (1, 2), (2, 4)))
    pattern = draw_pattern(jax.random.fold_in(key_of[4], 71), 0)
    return dict(queries=queries, keys=keys, values=values, pattern=pattern)


def attend_tile(query, keys, values):
    scores = jnp.einsum("qkgd,skd->kgqs", query, keys) * (HEAD_SIZE ** -0.5)
    top = jnp.max(scores, axis=-1, keepdims=True)
    weights = jnp.exp(scores - top)
    total = jnp.sum(weights, axis=-1)
    rounded = lax.optimization_barrier(weights.astype(jnp.bfloat16))
    mixed = jnp.einsum("kgqs,skd->kgqd", rounded.astype(jnp.float32), values)
    return mixed / total[..., None]


def reference(queries, keys, values, pattern):
    every_block_list = QB * DOCUMENT_COUNT
    query_block_list = queries.reshape(every_block_list, BLOCK_TOKENS, KEY_VALUE_HEADS, QUERY_HEADS // KEY_VALUE_HEADS, HEAD_SIZE).astype(jnp.float32)
    doc_index = (jnp.arange(every_block_list) // QB).astype(jnp.int32)
    chosen = pattern.reshape(every_block_list, SELECTED_BLOCKS).astype(jnp.int32)

    def one_block(items):
        query, document_number, picked_blocks = items
        document_keys = keys[document_number].reshape(CACHE_BLOCKS, BLOCK_TOKENS, KEY_VALUE_HEADS * HEAD_SIZE)
        document_values = values[document_number].reshape(CACHE_BLOCKS, BLOCK_TOKENS, KEY_VALUE_HEADS * HEAD_SIZE)
        key_row_list = document_keys[picked_blocks].reshape(SELECTED_BLOCKS * BLOCK_TOKENS, KEY_VALUE_HEADS, HEAD_SIZE).astype(jnp.float32)
        value_row_list = document_values[picked_blocks].reshape(SELECTED_BLOCKS * BLOCK_TOKENS, KEY_VALUE_HEADS, HEAD_SIZE).astype(jnp.float32)
        mixed = attend_tile(query, key_row_list, value_row_list)
        return jnp.transpose(mixed, (2, 0, 1, 3)).reshape(BLOCK_TOKENS, D).astype(jnp.bfloat16)

    attended = lax.map(one_block, (query_block_list, doc_index, chosen)).reshape(DOCUMENT_COUNT, QLEN, D)
    flat = attended.reshape(DOCUMENT_COUNT * QLEN, D)
    gram = jnp.dot(flat.T, flat, preferred_element_type=jnp.float32)
    return attended, gram
```

```python
import math

import jax
import jax.numpy as jnp
from jax import lax
from jax.experimental import pallas as pl
from jax.experimental.pallas import tpu as pltpu
from jax.sharding import PartitionSpec as P

HEAD_SIZE = 128
BLOCK_TOKENS = 128
NKB_DEV = 32
GROUP = 8
CAP = 12
PICKS = 16
QB = 2
NX = 4
NY = 4
NZ = 8
SLOTS = QB * CAP
SENT = 2 * SLOTS + GROUP
SCALE = HEAD_SIZE**-0.5 * math.log2(math.e)
BF16 = jnp.bfloat16
F32 = jnp.float32
ANY = pl.BlockSpec(memory_space=pl.ANY)
VMEM_LIMIT = 48 << 20


def hop(value, axis, step):
    if axis == "x":
        return lax.ppermute(value, "head", [(i, (i + step) % NX) for i in range(NX)])
    pairs = []
    for z in range(NZ):
        for y in range(NY):
            to_z = (z + step) % NZ if axis == "z" else z
            to_y = (y + step) % NY if axis == "y" else y
            pairs.append((z * NY + y, to_z * NY + to_y))
    return lax.ppermute(value, "doc", pairs)


def swap(value):
    return lax.ppermute(value, "ctx", [(0, 1), (1, 0)])


def pack_kernel(pattern, q, k, v, sent, sem):
    c = lax.axis_index("ctx")
    other = pl.multiple_of((1 - c) * HEAD_SIZE, HEAD_SIZE)

    def copies(act):
        for g in range(GROUP):
            at = pl.multiple_of((1 - c) * GROUP * HEAD_SIZE + g * HEAD_SIZE, HEAD_SIZE)
            act(pltpu.make_async_copy(q.at[:, pl.ds(at, HEAD_SIZE)], sent.at[2 * SLOTS + g], sem))
        for b in range(QB):
            count = 0
            for s in range(PICKS):
                block = pattern[b, s]
                mine = block // NKB_DEV == c
                row = pl.multiple_of((block % NKB_DEV) * BLOCK_TOKENS, BLOCK_TOKENS)
                slot = b * CAP + count

                @pl.when(mine)
                def _(row=row, slot=slot):
                    rows = pl.ds(row, BLOCK_TOKENS)
                    cols = pl.ds(other, HEAD_SIZE)
                    act(pltpu.make_async_copy(k.at[rows, cols], sent.at[slot], sem))
                    act(pltpu.make_async_copy(v.at[rows, cols], sent.at[SLOTS + slot], sem))

                count = count + mine.astype(jnp.int32)

    copies(lambda copy: copy.start())
    copies(lambda copy: copy.wait())


def pack(pattern, q, k, v):
    return pl.pallas_call(
        pack_kernel,
        out_shape=jax.ShapeDtypeStruct((SENT, BLOCK_TOKENS, HEAD_SIZE), BF16),
        in_specs=[pl.BlockSpec(memory_space=pltpu.SMEM), ANY, ANY, ANY],
        out_specs=ANY,
        scratch_shapes=[pltpu.SemaphoreType.DMA],
        name="pack",
    )(pattern, q, k, v)


def attend_kernel(pattern, q, k, v, got, own, lent, turned, qs, ks, vs, sems):
    c = lax.axis_index("ctx")
    mine_cols = pl.ds(pl.multiple_of(c * HEAD_SIZE, HEAD_SIZE), HEAD_SIZE)
    for b in range(QB):

        @pl.when(c == b)
        def _(b=b):
            for g in range(GROUP):
                at = pl.multiple_of(c * GROUP * HEAD_SIZE + g * HEAD_SIZE, HEAD_SIZE)
                pltpu.make_async_copy(q.at[:, pl.ds(at, HEAD_SIZE)], qs.at[b, g], sems.at[b, 0]).start()

        @pl.when(c != b)
        def _(b=b):
            pltpu.make_async_copy(got.at[pl.ds(2 * SLOTS, GROUP)], qs.at[b], sems.at[b, 0]).start()

        for kind, (cache, chosen) in enumerate(((k, ks), (v, vs))):
            count = 0
            for s in range(PICKS):
                block = pattern[b, s]
                mine = block // NKB_DEV == c
                row = pl.multiple_of((block % NKB_DEV) * BLOCK_TOKENS, BLOCK_TOKENS)
                slot = kind * SLOTS + b * CAP + count
                sem = sems.at[b, 1 + kind]

                @pl.when(mine)
                def _(row=row, s=s, cache=cache, chosen=chosen, sem=sem, b=b):
                    src = cache.at[pl.ds(row, BLOCK_TOKENS), mine_cols]
                    pltpu.make_async_copy(src, chosen.at[b, s], sem).start()

                @pl.when(jnp.logical_not(mine))
                def _(slot=slot, s=s, chosen=chosen, sem=sem, b=b):
                    pltpu.make_async_copy(got.at[slot], chosen.at[b, s], sem).start()

                count = count + 1 - mine.astype(jnp.int32)

    for b in range(QB):
        for i, chosen in enumerate((qs, ks, vs)):
            pltpu.make_async_copy(chosen.at[b], chosen.at[b], sems.at[b, i]).wait()
        keys = ks[b].reshape(PICKS * BLOCK_TOKENS, HEAD_SIZE)
        vals = vs[b].reshape(PICKS * BLOCK_TOKENS, HEAD_SIZE)
        for pair in range(GROUP // 2):
            rows = qs[b, 2 * pair : 2 * pair + 2].reshape(2 * BLOCK_TOKENS, HEAD_SIZE)
            scores = lax.dot_general(rows, keys, (((1,), (1,)), ((), ())), preferred_element_type=F32)
            top = jnp.max(scores, axis=-1, keepdims=True)
            weights = jnp.exp2((scores - top) * SCALE)
            total = jnp.sum(weights, axis=-1, keepdims=True)
            mixed = jnp.dot(weights.astype(BF16), vals, preferred_element_type=F32) / total
            for i in range(2):
                g = 2 * pair + i
                part = mixed[i * BLOCK_TOKENS : (i + 1) * BLOCK_TOKENS]
                cols = pl.ds(g * HEAD_SIZE, HEAD_SIZE)
                low = part.astype(BF16)

                @pl.when(c == b)
                def _(low=low, cols=cols):
                    own[:, cols] = low

                @pl.when(c != b)
                def _(low=low, cols=cols):
                    lent[:, cols] = low

                turned[cols, pl.ds(b * BLOCK_TOKENS, BLOCK_TOKENS)] = part.T.astype(BF16)


def attend(pattern, q, k, v, got):
    width = GROUP * HEAD_SIZE
    half = jax.ShapeDtypeStruct((BLOCK_TOKENS, width), BF16)
    chosen = pltpu.VMEM((QB, PICKS, BLOCK_TOKENS, HEAD_SIZE), BF16)
    vmem = pl.BlockSpec(memory_space=pltpu.VMEM)
    return pl.pallas_call(
        attend_kernel,
        out_shape=(half, half, jax.ShapeDtypeStruct((width, QB * BLOCK_TOKENS), BF16)),
        in_specs=[pl.BlockSpec(memory_space=pltpu.SMEM), ANY, ANY, ANY, ANY],
        out_specs=(vmem, vmem, vmem),
        scratch_shapes=[
            pltpu.VMEM((QB, GROUP, BLOCK_TOKENS, HEAD_SIZE), BF16),
            chosen,
            chosen,
            pltpu.SemaphoreType.DMA((QB, 3)),
        ],
        compiler_params=pltpu.CompilerParams(vmem_limit_bytes=VMEM_LIMIT),
        name="attend",
    )(pattern, q, k, v, got)


def product_kernel(n_a, n_b, *refs):
    a_in, b_in = refs[:n_a], refs[n_a : n_a + n_b]
    own, others, at, bt, sem_a, sem_b = refs[n_a + n_b :]
    c, x = lax.axis_index("ctx"), lax.axis_index("head")
    z = lax.axis_index("doc") // NY
    tok = QB * BLOCK_TOKENS
    copies = []
    for i, (ref, row, block) in enumerate(A_PIECES(a_in)):
        dst = at.at[pl.ds(row, ref.shape[0]), pl.ds(block * tok, tok)]
        copies.append(pltpu.make_async_copy(ref, dst, sem_a.at[i]))
    i = 0
    for ref, first, block in B_PIECES(b_in):
        for j in range(ref.shape[0]):
            dst = bt.at[first, :, pl.ds((block + j) * tok, tok)]
            copies.append(pltpu.make_async_copy(ref.at[j], dst, sem_b.at[i]))
            i += 1
    for copy in copies:
        copy.start()
    for copy in copies:
        copy.wait()
    left = at[...]
    for k in range(NZ):
        owner = lax.rem(z + k, NZ)
        away = lax.rem(owner // 2 + NX - x, NX)
        place = jnp.where(away == 0, 0, jnp.where(away == 3, 1, jnp.where(away == 1, 2, 3)))
        place = place + jnp.where(lax.rem(owner, 2) == c, 0, NX)
        made = lax.dot_general(left, bt[place], (((1,), (1,)), ((), ())), preferred_element_type=F32)
        if k == 0:
            own[...] = made
        else:
            others[k - 1] = made.astype(BF16)


def A_PIECES(refs):
    here, back, fore, far_top, far_low = refs
    return [(here, 0, 0), (back, 0, 1), (fore, 0, 2), (far_top, 0, 3), (far_low, far_top.shape[0], 3)]


def B_PIECES(refs):
    out = []
    for side in range(2):
        here, back, fore, far_top, far_low = refs[5 * side : 5 * side + 5]
        first = NX * side
        out += [(here, first, 0), (back, first + 1, 0), (fore, first + 2, 0)]
        out += [(far_top, first + 3, 0), (far_low, first + 3, 2)]
    return out


def products(a_pieces, b_pieces):
    width = GROUP * HEAD_SIZE
    cols = 2 * HEAD_SIZE
    tok = QB * BLOCK_TOKENS
    vmem = pl.BlockSpec(memory_space=pltpu.VMEM)
    n_b = sum(p.shape[0] for p in b_pieces)

    def body(*refs):
        product_kernel(len(a_pieces), len(b_pieces), *refs)

    return pl.pallas_call(
        body,
        out_shape=(
            jax.ShapeDtypeStruct((width, cols), F32),
            jax.ShapeDtypeStruct((NZ - 1, width, cols), BF16),
        ),
        in_specs=[ANY] * (len(a_pieces) + len(b_pieces)),
        out_specs=(vmem, vmem),
        scratch_shapes=[
            pltpu.VMEM((width, NY * tok), BF16),
            pltpu.VMEM((2 * NX, cols, NY * tok), BF16),
            pltpu.SemaphoreType.DMA((len(a_pieces),)),
            pltpu.SemaphoreType.DMA((n_b,)),
        ],
        compiler_params=pltpu.CompilerParams(vmem_limit_bytes=VMEM_LIMIT),
        name="products",
    )(*a_pieces, *b_pieces)


def added(got, here):
    return (got.astype(F32) + here.astype(F32)).astype(BF16)


def per_device(queries, keys, values, pattern):
    c = lax.axis_index("ctx")
    y = lax.axis_index("doc") % NY
    q, k, v, chosen = queries[0], keys[0], values[0], pattern[0]
    got = swap(pack(chosen, q, k, v))
    own, lent, turned = attend(chosen, q, k, v, got)
    cols = 2 * HEAD_SIZE

    def share(step):
        return lax.dynamic_slice_in_dim(turned, ((y + step) % NY) * cols, cols, 0)

    near = jnp.stack(
        [share(0), hop(share(1), "y", 1), hop(share(-1), "y", -1), hop(share(2), "y", 2)]
    )
    back, fore = hop(turned, "y", 1), hop(turned, "y", -1)
    half = turned.shape[0] // 2
    far_top, far_low = hop(back[:half], "y", 1), hop(fore[half:], "y", -1)
    x_back, x_fore = hop(near, "x", 1), hop(near, "x", -1)
    x_top, x_low = hop(x_back[:2], "x", 1), hop(x_fore[2:], "x", -1)
    b_pieces = [near, x_back, x_fore, x_top, x_low]
    b_pieces += [swap(p) for p in b_pieces]
    mine, others = products([turned, back, fore, far_top, far_low], b_pieces)

    def block(step, low):
        return others[step - 1, half:] if low else others[step - 1, :half]

    def chain(steps, low, direction):
        moved = hop(block(steps[0], low), "z", direction)
        for step in steps[1:]:
            moved = hop(added(moved, block(step, low)), "z", direction)
        return moved.astype(F32)

    top = chain((4, 3, 2, 1), False, 1) + chain((5, 6, 7), False, -1)
    low = chain((3, 2, 1), True, 1) + chain((4, 5, 6, 7), True, -1)
    gram = mine + jnp.concatenate([top, low], axis=0)

    returned = swap(lent)
    attended = jnp.where(
        c == 0,
        jnp.concatenate([own, returned], axis=1),
        jnp.concatenate([returned, own], axis=1),
    )
    return (attended[None], gram)


def solution(mesh):
    placed = (
        P("doc", "ctx", "head"),
        P("doc", "ctx", "head"),
        P("doc", "ctx", "head"),
        P("doc", None, None),
    )
    return jax.shard_map(
        per_device,
        mesh=mesh,
        in_specs=placed,
        out_specs=(P("doc", "ctx", "head"), P(("head", "ctx"), "doc")),
        check_vma=False,
    )
```

```python
import math

import jax
import jax.numpy as jnp
from jax import lax
from jax.experimental import pallas as pl
from jax.experimental.pallas import tpu as pltpu
from jax.sharding import PartitionSpec as P

HEAD_SIZE = 128
BLOCK_TOKENS = 128
NKB_DEV = 32
GROUP = 8
CAP = 12
PICKS = 16
QB = 2
NX = 4
NY = 4
NZ = 8
SLOTS = QB * CAP
SENT = 2 * SLOTS + GROUP
SCALE = HEAD_SIZE**-0.5 * math.log2(math.e)
BF16 = jnp.bfloat16
F32 = jnp.float32
ANY = pl.BlockSpec(memory_space=pl.ANY)


def hop(value, step):
    pairs = [(z * NY + y, z * NY + (y + step) % NY) for z in range(NZ) for y in range(NY)]
    return lax.ppermute(value, "doc", pairs)


def toward(value, axis):
    pairs = []
    if axis == "x":
        for c, step in ((0, 1), (1, -1)):
            pairs += [(c * NX + x, c * NX + (x + step) % NX) for x in range(NX)]
        return lax.ppermute(value, ("ctx", "head"), pairs)
    for c, step in ((0, 1), (1, -1)):
        for z in range(NZ):
            for y in range(NY):
                to_z = (z + step) % NZ if axis == "z" else z
                to_y = (y + step) % NY if axis == "y" else y
                pairs.append(((c * NZ + z) * NY + y, (c * NZ + to_z) * NY + to_y))
    return lax.ppermute(value, ("ctx", "doc"), pairs)


def swap(value):
    return lax.ppermute(value, "ctx", [(0, 1), (1, 0)])


def pack_kernel(pattern, q, k, v, sent, sem):
    c = lax.axis_index("ctx")
    other = pl.multiple_of((1 - c) * HEAD_SIZE, HEAD_SIZE)

    def copies(act):
        for g in range(GROUP):
            at = pl.multiple_of((1 - c) * GROUP * HEAD_SIZE + g * HEAD_SIZE, HEAD_SIZE)
            act(pltpu.make_async_copy(q.at[:, pl.ds(at, HEAD_SIZE)], sent.at[2 * SLOTS + g], sem))
        for b in range(QB):
            count = 0
            for s in range(PICKS):
                block = pattern[b, s]
                mine = block // NKB_DEV == c
                row = pl.multiple_of((block % NKB_DEV) * BLOCK_TOKENS, BLOCK_TOKENS)
                slot = b * CAP + count

                @pl.when(mine)
                def _(row=row, slot=slot):
                    rows = pl.ds(row, BLOCK_TOKENS)
                    cols = pl.ds(other, HEAD_SIZE)
                    act(pltpu.make_async_copy(k.at[rows, cols], sent.at[slot], sem))
                    act(pltpu.make_async_copy(v.at[rows, cols], sent.at[SLOTS + slot], sem))

                count = count + mine.astype(jnp.int32)

    copies(lambda copy: copy.start())
    copies(lambda copy: copy.wait())


def pack(pattern, q, k, v):
    return pl.pallas_call(
        pack_kernel,
        out_shape=jax.ShapeDtypeStruct((SENT, BLOCK_TOKENS, HEAD_SIZE), BF16),
        in_specs=[pl.BlockSpec(memory_space=pltpu.SMEM), ANY, ANY, ANY],
        out_specs=pl.BlockSpec(memory_space=pltpu.VMEM),
        scratch_shapes=[pltpu.SemaphoreType.DMA],
        name="pack",
    )(pattern, q, k, v)


def attend_kernel(pattern, q, k, v, got, out, turned, qs, ks, vs, sems):
    c = lax.axis_index("ctx")
    mine_cols = pl.ds(pl.multiple_of(c * HEAD_SIZE, HEAD_SIZE), HEAD_SIZE)
    for b in range(QB):

        @pl.when(c == b)
        def _(b=b):
            for g in range(GROUP):
                at = pl.multiple_of(c * GROUP * HEAD_SIZE + g * HEAD_SIZE, HEAD_SIZE)
                pltpu.make_async_copy(q.at[:, pl.ds(at, HEAD_SIZE)], qs.at[b, g], sems.at[b, 0]).start()

        @pl.when(c != b)
        def _(b=b):
            pltpu.make_async_copy(got.at[pl.ds(2 * SLOTS, GROUP)], qs.at[b], sems.at[b, 0]).start()

        for kind, (cache, chosen) in enumerate(((k, ks), (v, vs))):
            count = 0
            for s in range(PICKS):
                block = pattern[b, s]
                mine = block // NKB_DEV == c
                row = pl.multiple_of((block % NKB_DEV) * BLOCK_TOKENS, BLOCK_TOKENS)
                slot = kind * SLOTS + b * CAP + count
                sem = sems.at[b, 1 + kind]

                @pl.when(mine)
                def _(row=row, s=s, cache=cache, chosen=chosen, sem=sem, b=b):
                    src = cache.at[pl.ds(row, BLOCK_TOKENS), mine_cols]
                    pltpu.make_async_copy(src, chosen.at[b, s], sem).start()

                @pl.when(jnp.logical_not(mine))
                def _(slot=slot, s=s, chosen=chosen, sem=sem, b=b):
                    pltpu.make_async_copy(got.at[slot], chosen.at[b, s], sem).start()

                count = count + 1 - mine.astype(jnp.int32)

    for b in range(QB):
        for i, chosen in enumerate((qs, ks, vs)):
            pltpu.make_async_copy(chosen.at[b], chosen.at[b], sems.at[b, i]).wait()
        keys = ks[b].reshape(PICKS * BLOCK_TOKENS, HEAD_SIZE)
        vals = vs[b].reshape(PICKS * BLOCK_TOKENS, HEAD_SIZE)
        for pair in range(GROUP // 2):
            rows = qs[b, 2 * pair : 2 * pair + 2].reshape(2 * BLOCK_TOKENS, HEAD_SIZE)
            scores = lax.dot_general(rows, keys, (((1,), (1,)), ((), ())), preferred_element_type=F32)
            top = jnp.max(scores, axis=-1, keepdims=True)
            weights = jnp.exp2((scores - top) * SCALE)
            total = jnp.sum(weights, axis=-1, keepdims=True)
            mixed = jnp.dot(weights.astype(BF16), vals, preferred_element_type=F32) / total
            for i in range(2):
                g = 2 * pair + i
                part = mixed[i * BLOCK_TOKENS : (i + 1) * BLOCK_TOKENS]
                cols = pl.ds(g * HEAD_SIZE, HEAD_SIZE)
                out[jnp.where(c == b, 0, 1), :, cols] = part.astype(BF16)
                turned[cols, pl.ds(b * BLOCK_TOKENS, BLOCK_TOKENS)] = part.T.astype(BF16)


def attend(pattern, q, k, v, got):
    width = GROUP * HEAD_SIZE
    out = jax.ShapeDtypeStruct((QB, BLOCK_TOKENS, width), BF16)
    chosen = pltpu.VMEM((QB, PICKS, BLOCK_TOKENS, HEAD_SIZE), BF16)
    vmem = pl.BlockSpec(memory_space=pltpu.VMEM)
    return pl.pallas_call(
        attend_kernel,
        out_shape=(out, jax.ShapeDtypeStruct((width, QB * BLOCK_TOKENS), BF16)),
        in_specs=[pl.BlockSpec(memory_space=pltpu.SMEM), ANY, ANY, ANY, ANY],
        out_specs=(vmem, vmem),
        scratch_shapes=[
            pltpu.VMEM((QB, GROUP, BLOCK_TOKENS, HEAD_SIZE), BF16),
            chosen,
            chosen,
            pltpu.SemaphoreType.DMA((QB, 3)),
        ],
        compiler_params=pltpu.CompilerParams(vmem_limit_bytes=32 << 20),
        name="attend",
    )(pattern, q, k, v, got)


def right_part(refs, case, r):
    near, x1, x1_other, x2, x2_other = refs
    if case == 0:
        return near[r]
    if case == 1:
        return x1[r]
    if case == 2:
        return x1_other[1 - r]
    return (x2, x2_other)[r][...]


def product_kernel(tasks, *refs):
    both, y1, y1_other, y2, y2_other = refs[:5]
    rights, outs, bt = refs[5:10], refs[10:-1], refs[-1]
    c, x = lax.axis_index("ctx"), lax.axis_index("head")
    z = lax.axis_index("doc") // NY
    for i in sorted({i for i, _ in tasks}):
        owner = lax.rem(z + jnp.where(c == 0, 4 - i, 4 + i), NZ)
        away = lax.rem(owner // 2 + NX - x, NX)
        other = (lax.rem(owner, 2) != c).astype(jnp.int32)
        side = jnp.where(c == 0, 3, 1)
        case = jnp.where(away == 0, 0, jnp.where(away == 2, 3, jnp.where(away == side, 1, 2)))
        for k in range(4):
            for r in range(2):

                @pl.when(jnp.logical_and(case == k, other == r))
                def _(k=k, r=r):
                    bt[...] = right_part(rights, k, r)

        for r in sorted({r for j, r in tasks if j == i}):
            total = None
            lefts = (both[r], y1[r], y1_other[1 - r], (y2, y2_other)[r][...])
            for left, doc in zip(lefts, (0, 1 + c, 2 - c, 3)):
                dims = (((1,), (1,)), ((), ()))
                term = lax.dot_general(left, bt[doc], dims, preferred_element_type=F32)
                total = term if total is None else total + term
            out = outs[tasks.index((i, r))]
            out[...] = total.astype(out.dtype)


def products(tasks, lefts, rights):
    rows, cols = GROUP * HEAD_SIZE, 2 * HEAD_SIZE
    vmem = pl.BlockSpec(memory_space=pltpu.VMEM)

    def body(*refs):
        product_kernel(tasks, *refs)

    return pl.pallas_call(
        body,
        out_shape=[jax.ShapeDtypeStruct((rows, cols), F32 if i == 4 else BF16) for i, _ in tasks],
        in_specs=[vmem] * 10,
        out_specs=[vmem] * len(tasks),
        scratch_shapes=[pltpu.VMEM((NY, cols, QB * BLOCK_TOKENS), BF16)],
        compiler_params=pltpu.CompilerParams(vmem_limit_bytes=16 << 20),
        name="products",
    )(*lefts, *rights)


def added(got, here):
    return (got.astype(F32) + here.astype(F32)).astype(BF16)


def per_device(queries, keys, values, pattern):
    c = lax.axis_index("ctx")
    y = lax.axis_index("doc") % NY
    q, k, v, chosen = queries[0], keys[0], values[0], pattern[0]
    got = swap(pack(chosen, q, k, v))
    out, turned = attend(chosen, q, k, v, got)
    cols = 2 * HEAD_SIZE

    def share(step):
        return lax.dynamic_slice_in_dim(turned, ((y + step) % NY) * cols, cols, 0)

    mine = jnp.stack([share(0), hop(share(1), 1), hop(share(-1), -1), hop(share(2), 2)])
    both = jnp.stack([turned, swap(turned)])
    near = jnp.stack([mine, swap(mine)])
    y1 = toward(both, "y")
    x1 = toward(near, "x")
    x2 = toward(x1[0], "x")
    y2 = toward(y1[0], "y")
    lefts = [both, y1, swap(y1), y2, swap(y2)]
    rights = [near, x1, swap(x1), x2, swap(x2)]

    [first] = products([(0, 0)], lefts, rights)
    second = products([(1, 0), (1, 1)], lefts, rights)
    third = products([(2, 0), (2, 1), (3, 0), (3, 1), (4, 0)], lefts, rights)
    long = toward(first, "z")
    short = toward(second[1], "z")
    long = toward(added(long, second[0]), "z")
    short = toward(added(short, third[1]), "z")
    long = toward(added(long, third[0]), "z")
    short = toward(added(short, third[3]), "z")
    long = toward(added(long, third[2]), "z")
    gram = third[4] + swap(short).astype(F32) + long.astype(F32)

    own, returned = out[0], swap(out[1])
    attended = jnp.where(
        c == 0,
        jnp.concatenate([own, returned], axis=1),
        jnp.concatenate([returned, own], axis=1),
    )
    return (attended[None], gram)


def solution(mesh):
    placed = (
        P("doc", "ctx", "head"),
        P("doc", "ctx", "head"),
        P("doc", "ctx", "head"),
        P("doc", None, None),
    )
    return jax.shard_map(
        per_device,
        mesh=mesh,
        in_specs=placed,
        out_specs=(P("doc", "ctx", "head"), P(("head", "ctx"), "doc")),
        check_vma=False,
    )
```

```python
import math

import jax
import jax.numpy as jnp
from jax import lax
from jax.experimental import pallas as pl
from jax.experimental.pallas import tpu as pltpu
from jax.sharding import PartitionSpec as P

HEAD_SIZE = 128
BLOCK_TOKENS = 128
NKB_DEV = 32
GROUP = 8
CAP = 12
PICKS = 16
QB = 2
NX = 4
NY = 4
NZ = 8
SLOTS = QB * CAP
SENT = 2 * SLOTS + GROUP
SCALE = HEAD_SIZE**-0.5 * math.log2(math.e)
BF16 = jnp.bfloat16
F32 = jnp.float32
ANY = pl.BlockSpec(memory_space=pl.ANY)


def hop(value, step):
    pairs = [(z * NY + y, z * NY + (y + step) % NY) for z in range(NZ) for y in range(NY)]
    return lax.ppermute(value, "doc", pairs)


def toward(value, axis):
    pairs = []
    if axis == "x":
        for c, step in ((0, 1), (1, -1)):
            pairs += [(c * NX + x, c * NX + (x + step) % NX) for x in range(NX)]
        return lax.ppermute(value, ("ctx", "head"), pairs)
    for c, step in ((0, 1), (1, -1)):
        for z in range(NZ):
            for y in range(NY):
                to_z = (z + step) % NZ if axis == "z" else z
                to_y = (y + step) % NY if axis == "y" else y
                pairs.append(((c * NZ + z) * NY + y, (c * NZ + to_z) * NY + to_y))
    return lax.ppermute(value, ("ctx", "doc"), pairs)


def swap(value):
    return lax.ppermute(value, "ctx", [(0, 1), (1, 0)])


def pack_kernel(away, pattern, q, k, v, packed, sem):
    c = lax.axis_index("ctx")
    head = 1 - c if away else c
    cols = pl.ds(pl.multiple_of(head * HEAD_SIZE, HEAD_SIZE), HEAD_SIZE)
    for g in range(GROUP):
        at = pl.multiple_of(head * GROUP * HEAD_SIZE + g * HEAD_SIZE, HEAD_SIZE)
        pltpu.make_async_copy(q.at[:, pl.ds(at, HEAD_SIZE)], packed.at[2 * SLOTS + g], sem).start()
    many = 0
    for b in range(QB):
        count = 0
        for s in range(PICKS):
            block = pattern[b, s]
            mine = block // NKB_DEV == c
            row = pl.multiple_of((block % NKB_DEV) * BLOCK_TOKENS, BLOCK_TOKENS)
            slot = b * CAP + count

            @pl.when(mine)
            def _(row=row, slot=slot):
                rows = pl.ds(row, BLOCK_TOKENS)
                pltpu.make_async_copy(k.at[rows, cols], packed.at[slot], sem).start()
                pltpu.make_async_copy(v.at[rows, cols], packed.at[SLOTS + slot], sem).start()

            count = count + mine.astype(jnp.int32)
        many = many + count

    queries = packed.at[pl.ds(2 * SLOTS, GROUP)]
    pltpu.make_async_copy(queries, queries, sem).wait()

    def settle(_, carry):
        pair = packed.at[pl.ds(0, 2)]
        pltpu.make_async_copy(pair, pair, sem).wait()
        return carry

    lax.fori_loop(0, many, settle, 0)


def pack(away, pattern, q, k, v):
    def body(*refs):
        pack_kernel(away, *refs)

    return pl.pallas_call(
        body,
        out_shape=jax.ShapeDtypeStruct((SENT, BLOCK_TOKENS, HEAD_SIZE), BF16),
        in_specs=[pl.BlockSpec(memory_space=pltpu.SMEM), ANY, ANY, ANY],
        out_specs=pl.BlockSpec(memory_space=pltpu.VMEM),
        scratch_shapes=[pltpu.SemaphoreType.DMA],
        name="pack_away" if away else "pack_here",
    )(pattern, q, k, v)


def attend_kernel(pattern, kept, got, out, turned, qs, ks, vs):
    c = lax.axis_index("ctx")
    for b in range(QB):
        count = 0
        for s in range(PICKS):
            count = count + (pattern[b, s] // NKB_DEV == c).astype(jnp.int32)
        for kind, chosen in enumerate((ks, vs)):
            slots = pl.ds(kind * SLOTS + b * CAP, CAP)
            chosen[b, pl.ds(0, CAP)] = kept[slots]
            chosen[b, pl.ds(count, CAP)] = got[slots]
        for source, here in ((kept, c == b), (got, c != b)):

            @pl.when(here)
            def _(source=source, b=b):
                qs[b] = source[pl.ds(2 * SLOTS, GROUP)]

    for b in range(QB):
        keys = ks[b, :PICKS].reshape(PICKS * BLOCK_TOKENS, HEAD_SIZE)
        vals = vs[b, :PICKS].reshape(PICKS * BLOCK_TOKENS, HEAD_SIZE)
        for pair in range(GROUP // 2):
            rows = qs[b, 2 * pair : 2 * pair + 2].reshape(2 * BLOCK_TOKENS, HEAD_SIZE)
            scores = lax.dot_general(rows, keys, (((1,), (1,)), ((), ())), preferred_element_type=F32)
            top = jnp.max(scores, axis=-1, keepdims=True)
            weights = jnp.exp2((scores - top) * SCALE)
            total = jnp.sum(weights, axis=-1, keepdims=True)
            mixed = jnp.dot(weights.astype(BF16), vals, preferred_element_type=F32) / total
            for i in range(2):
                g = 2 * pair + i
                part = mixed[i * BLOCK_TOKENS : (i + 1) * BLOCK_TOKENS]
                cols = pl.ds(g * HEAD_SIZE, HEAD_SIZE)
                out[jnp.where(c == b, 0, 1), :, cols] = part.astype(BF16)
                turned[cols, pl.ds(b * BLOCK_TOKENS, BLOCK_TOKENS)] = part.T.astype(BF16)


def attend(pattern, kept, got):
    width = GROUP * HEAD_SIZE
    out = jax.ShapeDtypeStruct((QB, BLOCK_TOKENS, width), BF16)
    chosen = pltpu.VMEM((QB, 2 * CAP, BLOCK_TOKENS, HEAD_SIZE), BF16)
    vmem = pl.BlockSpec(memory_space=pltpu.VMEM)
    return pl.pallas_call(
        attend_kernel,
        out_shape=(out, jax.ShapeDtypeStruct((width, QB * BLOCK_TOKENS), BF16)),
        in_specs=[pl.BlockSpec(memory_space=pltpu.SMEM), vmem, vmem],
        out_specs=(vmem, vmem),
        scratch_shapes=[
            pltpu.VMEM((QB, GROUP, BLOCK_TOKENS, HEAD_SIZE), BF16),
            chosen,
            chosen,
        ],
        compiler_params=pltpu.CompilerParams(vmem_limit_bytes=32 << 20),
        name="attend",
    )(pattern, kept, got)


def product_kernel(tasks, *refs):
    lefts = refs[:4], refs[4:8]
    rights = tuple(zip(refs[8:12], refs[12:16]))
    outs, bt = refs[16:-1], refs[-1]
    c, x = lax.axis_index("ctx"), lax.axis_index("head")
    z = lax.axis_index("doc") // NY
    for i in sorted({i for i, _ in tasks}):
        owner = lax.rem(z + jnp.where(c == 0, 4 - i, 4 + i), NZ)
        away = lax.rem(owner // 2 + NX - x, NX)
        other = (lax.rem(owner, 2) != c).astype(jnp.int32)
        side = jnp.where(c == 0, 3, 1)
        case = jnp.where(away == 0, 0, jnp.where(away == 2, 3, jnp.where(away == side, 1, 2)))
        for k in range(4):
            for r in range(2):

                @pl.when(jnp.logical_and(case == k, other == r))
                def _(k=k, r=r):
                    bt[...] = rights[k][r][...]

        for r in sorted({r for j, r in tasks if j == i}):
            total = None
            for left, doc in zip(lefts[r], (0, 1 + c, 2 - c, 3)):
                dims = (((1,), (1,)), ((), ()))
                term = lax.dot_general(left[...], bt[doc], dims, preferred_element_type=F32)
                total = term if total is None else total + term
            out = outs[tasks.index((i, r))]
            out[...] = total.astype(out.dtype)


def products(tasks, lefts, rights):
    rows, cols = GROUP * HEAD_SIZE, 2 * HEAD_SIZE
    vmem = pl.BlockSpec(memory_space=pltpu.VMEM)

    def body(*refs):
        product_kernel(tasks, *refs)

    return pl.pallas_call(
        body,
        out_shape=[jax.ShapeDtypeStruct((rows, cols), F32 if i == 4 else BF16) for i, _ in tasks],
        in_specs=[vmem] * 16,
        out_specs=[vmem] * len(tasks),
        scratch_shapes=[pltpu.VMEM((NY, cols, QB * BLOCK_TOKENS), BF16)],
        compiler_params=pltpu.CompilerParams(vmem_limit_bytes=16 << 20),
        name="products",
    )(*lefts[0], *lefts[1], *rights[0], *rights[1])


def added(got, here):
    return (got.astype(F32) + here.astype(F32)).astype(BF16)


def per_device(queries, keys, values, pattern):
    c = lax.axis_index("ctx")
    y = lax.axis_index("doc") % NY
    q, k, v, chosen = queries[0], keys[0], values[0], pattern[0]
    got = swap(pack(True, chosen, q, k, v))
    kept = pack(False, chosen, q, k, v)
    out, turned = attend(chosen, kept, got)
    cols = 2 * HEAD_SIZE

    def share(step):
        return lax.dynamic_slice_in_dim(turned, ((y + step) % NY) * cols, cols, 0)

    mine = jnp.stack([share(0), hop(share(1), 1), hop(share(-1), -1), hop(share(2), 2)])
    x1 = toward(mine, "x")
    y1 = toward(turned, "y")
    mine_other, turned_other = swap(mine), swap(turned)
    x1_other, y1_other = toward(mine_other, "x"), toward(turned_other, "y")
    x2, y2 = toward(x1, "x"), toward(y1, "y")
    lefts = [turned, y1, swap(y1_other), y2], [turned_other, y1_other, swap(y1), swap(y2)]
    rights = [mine, x1, swap(x1_other), x2], [mine_other, x1_other, swap(x1), swap(x2)]

    [first] = products([(0, 0)], lefts, rights)
    second = products([(1, 0), (1, 1)], lefts, rights)
    third = products([(2, 0), (2, 1), (3, 0), (3, 1), (4, 0)], lefts, rights)
    long = toward(first, "z")
    short = toward(second[1], "z")
    long = toward(added(long, second[0]), "z")
    short = toward(added(short, third[1]), "z")
    long = toward(added(long, third[0]), "z")
    short = toward(added(short, third[3]), "z")
    long = toward(added(long, third[2]), "z")
    gram = third[4] + swap(short).astype(F32) + long.astype(F32)

    own, returned = out[0], swap(out[1])
    attended = jnp.where(
        c == 0,
        jnp.concatenate([own, returned], axis=1),
        jnp.concatenate([returned, own], axis=1),
    )
    return (attended[None], gram)


def solution(mesh):
    placed = (
        P("doc", "ctx", "head"),
        P("doc", "ctx", "head"),
        P("doc", "ctx", "head"),
        P("doc", None, None),
    )
    return jax.shard_map(
        per_device,
        mesh=mesh,
        in_specs=placed,
        out_specs=(P("doc", "ctx", "head"), P(("head", "ctx"), "doc")),
        check_vma=False,
    )
```

```python
import math

import jax
import jax.numpy as jnp
from jax import lax
from jax.experimental import pallas as pl
from jax.experimental.pallas import tpu as pltpu
from jax.sharding import PartitionSpec as P

HEAD_SIZE = 128
BLOCK_TOKENS = 128
NKB_DEV = 32
GROUP = 8
CAP = 12
PICKS = 16
QB = 2
NX = 4
NY = 4
NZ = 8
SLOTS = QB * CAP
SENT = 2 * SLOTS + GROUP
SCALE = HEAD_SIZE**-0.5 * math.log2(math.e)
BF16 = jnp.bfloat16
F32 = jnp.float32
ANY = pl.BlockSpec(memory_space=pl.ANY)


def hop(value, step):
    pairs = [(z * NY + y, z * NY + (y + step) % NY) for z in range(NZ) for y in range(NY)]
    return lax.ppermute(value, "doc", pairs)


def toward(value, axis):
    pairs = []
    if axis == "x":
        for c, step in ((0, 1), (1, -1)):
            pairs += [(c * NX + x, c * NX + (x + step) % NX) for x in range(NX)]
        return lax.ppermute(value, ("ctx", "head"), pairs)
    for c, step in ((0, 1), (1, -1)):
        for z in range(NZ):
            for y in range(NY):
                to_z = (z + step) % NZ if axis == "z" else z
                to_y = (y + step) % NY if axis == "y" else y
                pairs.append(((c * NZ + z) * NY + y, (c * NZ + to_z) * NY + to_y))
    return lax.ppermute(value, ("ctx", "doc"), pairs)


def swap(value):
    return lax.ppermute(value, "ctx", [(0, 1), (1, 0)])


def pack_kernel(away, pattern, q, k, v, packed, sem):
    c = lax.axis_index("ctx")
    head = 1 - c if away else c
    cols = pl.ds(pl.multiple_of(head * HEAD_SIZE, HEAD_SIZE), HEAD_SIZE)
    for g in range(GROUP):
        at = pl.multiple_of(head * GROUP * HEAD_SIZE + g * HEAD_SIZE, HEAD_SIZE)
        pltpu.make_async_copy(q.at[:, pl.ds(at, HEAD_SIZE)], packed.at[2 * SLOTS + g], sem).start()
    many = 0
    for b in range(QB):
        count = 0
        for s in range(PICKS):
            block = pattern[b, s]
            mine = block // NKB_DEV == c
            row = pl.multiple_of((block % NKB_DEV) * BLOCK_TOKENS, BLOCK_TOKENS)
            slot = b * CAP + count

            @pl.when(mine)
            def _(row=row, slot=slot):
                rows = pl.ds(row, BLOCK_TOKENS)
                pltpu.make_async_copy(k.at[rows, cols], packed.at[slot], sem).start()
                pltpu.make_async_copy(v.at[rows, cols], packed.at[SLOTS + slot], sem).start()

            count = count + mine.astype(jnp.int32)
        many = many + count

    queries = packed.at[pl.ds(2 * SLOTS, GROUP)]
    pltpu.make_async_copy(queries, queries, sem).wait()

    def settle(_, carry):
        pair = packed.at[pl.ds(0, 2)]
        pltpu.make_async_copy(pair, pair, sem).wait()
        return carry

    lax.fori_loop(0, many, settle, 0)


def pack(away, pattern, q, k, v):
    def body(*refs):
        pack_kernel(away, *refs)

    return pl.pallas_call(
        body,
        out_shape=jax.ShapeDtypeStruct((SENT, BLOCK_TOKENS, HEAD_SIZE), BF16),
        in_specs=[pl.BlockSpec(memory_space=pltpu.SMEM), ANY, ANY, ANY],
        out_specs=pl.BlockSpec(memory_space=pltpu.VMEM),
        scratch_shapes=[pltpu.SemaphoreType.DMA],
        name="pack_away" if away else "pack_here",
    )(pattern, q, k, v)


def attend_kernel(pattern, kept, got, out, turned, qs, ks, vs):
    c = lax.axis_index("ctx")
    for b in range(QB):
        count = 0
        for s in range(PICKS):
            count = count + (pattern[b, s] // NKB_DEV == c).astype(jnp.int32)
        for kind, chosen in enumerate((ks, vs)):
            slots = pl.ds(kind * SLOTS + b * CAP, CAP)
            chosen[b, pl.ds(0, CAP)] = kept[slots]
            chosen[b, pl.ds(count, CAP)] = got[slots]
        for source, here in ((kept, c == b), (got, c != b)):

            @pl.when(here)
            def _(source=source, b=b):
                qs[b] = source[pl.ds(2 * SLOTS, GROUP)]

    for b in range(QB):
        keys = ks[b, :PICKS].reshape(PICKS * BLOCK_TOKENS, HEAD_SIZE)
        vals = vs[b, :PICKS].reshape(PICKS * BLOCK_TOKENS, HEAD_SIZE)
        for pair in range(GROUP // 2):
            rows = qs[b, 2 * pair : 2 * pair + 2].reshape(2 * BLOCK_TOKENS, HEAD_SIZE)
            scores = lax.dot_general(rows, keys, (((1,), (1,)), ((), ())), preferred_element_type=F32)
            top = jnp.max(scores, axis=-1, keepdims=True)
            weights = jnp.exp2((scores - top) * SCALE)
            total = jnp.sum(weights, axis=-1, keepdims=True)
            mixed = jnp.dot(weights.astype(BF16), vals, preferred_element_type=F32) / total
            for i in range(2):
                g = 2 * pair + i
                part = mixed[i * BLOCK_TOKENS : (i + 1) * BLOCK_TOKENS]
                cols = pl.ds(g * HEAD_SIZE, HEAD_SIZE)
                out[jnp.where(c == b, 0, 1), :, cols] = part.astype(BF16)
                turned[cols, pl.ds(b * BLOCK_TOKENS, BLOCK_TOKENS)] = part.T.astype(BF16)


def attend(pattern, kept, got):
    width = GROUP * HEAD_SIZE
    out = jax.ShapeDtypeStruct((QB, BLOCK_TOKENS, width), BF16)
    chosen = pltpu.VMEM((QB, 2 * CAP, BLOCK_TOKENS, HEAD_SIZE), BF16)
    vmem = pl.BlockSpec(memory_space=pltpu.VMEM)
    return pl.pallas_call(
        attend_kernel,
        out_shape=(out, jax.ShapeDtypeStruct((width, QB * BLOCK_TOKENS), BF16)),
        in_specs=[pl.BlockSpec(memory_space=pltpu.SMEM), vmem, vmem],
        out_specs=(vmem, vmem),
        scratch_shapes=[
            pltpu.VMEM((QB, GROUP, BLOCK_TOKENS, HEAD_SIZE), BF16),
            chosen,
            chosen,
        ],
        compiler_params=pltpu.CompilerParams(vmem_limit_bytes=32 << 20),
        name="attend",
    )(pattern, kept, got)


def product_kernel(tasks, *refs):
    lefts = refs[:4], refs[4:8]
    rights = tuple(zip(refs[8:12], refs[12:16]))
    outs, bt = refs[16:-1], refs[-1]
    c, x = lax.axis_index("ctx"), lax.axis_index("head")
    z = lax.axis_index("doc") // NY
    for i in sorted({i for i, _ in tasks}):
        owner = lax.rem(z + jnp.where(c == 0, 4 - i, 4 + i), NZ)
        away = lax.rem(owner // 2 + NX - x, NX)
        other = (lax.rem(owner, 2) != c).astype(jnp.int32)
        side = jnp.where(c == 0, 3, 1)
        case = jnp.where(away == 0, 0, jnp.where(away == 2, 3, jnp.where(away == side, 1, 2)))
        for k in range(4):
            for r in range(2):

                @pl.when(jnp.logical_and(case == k, other == r))
                def _(k=k, r=r):
                    bt[...] = rights[k][r][...]

        for r in sorted({r for j, r in tasks if j == i}):
            total = None
            for left, doc in zip(lefts[r], (0, 1 + c, 2 - c, 3)):
                dims = (((1,), (1,)), ((), ()))
                term = lax.dot_general(left[...], bt[doc], dims, preferred_element_type=F32)
                total = term if total is None else total + term
            out = outs[tasks.index((i, r))]
            out[...] = total.astype(out.dtype)


def products(tasks, lefts, rights):
    rows, cols = GROUP * HEAD_SIZE, 2 * HEAD_SIZE
    vmem = pl.BlockSpec(memory_space=pltpu.VMEM)

    def body(*refs):
        product_kernel(tasks, *refs)

    return pl.pallas_call(
        body,
        out_shape=[jax.ShapeDtypeStruct((rows, cols), F32 if i == 4 else BF16) for i, _ in tasks],
        in_specs=[vmem] * 16,
        out_specs=[vmem] * len(tasks),
        scratch_shapes=[pltpu.VMEM((NY, cols, QB * BLOCK_TOKENS), BF16)],
        compiler_params=pltpu.CompilerParams(vmem_limit_bytes=16 << 20),
        name="products",
    )(*lefts[0], *lefts[1], *rights[0], *rights[1])


def added(got, here):
    return (got.astype(F32) + here.astype(F32)).astype(BF16)


def per_device(queries, keys, values, pattern):
    c = lax.axis_index("ctx")
    y = lax.axis_index("doc") % NY
    q, k, v, chosen = queries[0], keys[0], values[0], pattern[0]
    got = swap(pack(True, chosen, q, k, v))
    kept = pack(False, chosen, q, k, v)
    out, turned = attend(chosen, kept, got)
    cols = 2 * HEAD_SIZE

    def share(step):
        return lax.dynamic_slice_in_dim(turned, ((y + step) % NY) * cols, cols, 0)

    mine = jnp.stack([share(0), hop(share(1), 1), hop(share(-1), -1), hop(share(2), 2)])
    x1 = toward(mine, "x")
    y1 = toward(turned, "y")
    mine_other, turned_other = swap(mine), swap(turned)
    x1_other, y1_other = toward(mine_other, "x"), toward(turned_other, "y")
    x2, y2 = toward(x1, "x"), toward(y1, "y")
    lefts = [turned, y1, swap(y1_other), y2], [turned_other, y1_other, swap(y1), swap(y2)]
    rights = [mine, x1, swap(x1_other), x2], [mine_other, x1_other, swap(x1), swap(x2)]

    [first] = products([(0, 0)], lefts, rights)
    second = products([(1, 0), (1, 1)], lefts, rights)
    third = products([(2, 0), (2, 1), (3, 0), (3, 1), (4, 0)], lefts, rights)
    long = toward(first, "z")
    short = toward(second[1], "z")
    here, third = lax.optimization_barrier((second[0], third))
    long = toward(added(long, here), "z")
    short = toward(added(short, third[1]), "z")
    long = toward(added(long, third[0]), "z")
    short = toward(added(short, third[3]), "z")
    long = toward(added(long, third[2]), "z")
    gram = third[4] + swap(short).astype(F32) + long.astype(F32)

    own, returned = out[0], swap(out[1])
    attended = jnp.where(
        c == 0,
        jnp.concatenate([own, returned], axis=1),
        jnp.concatenate([returned, own], axis=1),
    )
    return (attended[None], gram)


def solution(mesh):
    placed = (
        P("doc", "ctx", "head"),
        P("doc", "ctx", "head"),
        P("doc", "ctx", "head"),
        P("doc", None, None),
    )
    return jax.shard_map(
        per_device,
        mesh=mesh,
        in_specs=placed,
        out_specs=(P("doc", "ctx", "head"), P(("head", "ctx"), "doc")),
        check_vma=False,
    )
```

```python
import math

import jax
import jax.numpy as jnp
from jax import lax
from jax.experimental import pallas as pl
from jax.experimental.pallas import tpu as pltpu
from jax.sharding import PartitionSpec as P

HEAD_SIZE = 128
BLOCK_TOKENS = 128
NKB_DEV = 32
GROUP = 8
CAP = 12
PICKS = 16
QB = 2
NX = 4
NY = 4
NZ = 8
SLOTS = QB * CAP
SENT = 2 * SLOTS + GROUP
SCALE = HEAD_SIZE**-0.5 * math.log2(math.e)
BF16 = jnp.bfloat16
F32 = jnp.float32
ANY = pl.BlockSpec(memory_space=pl.ANY)


def hop(value, step):
    pairs = [(z * NY + y, z * NY + (y + step) % NY) for z in range(NZ) for y in range(NY)]
    return lax.ppermute(value, "doc", pairs)


def toward(value, axis):
    pairs = []
    if axis == "x":
        for c, step in ((0, 1), (1, -1)):
            pairs += [(c * NX + x, c * NX + (x + step) % NX) for x in range(NX)]
        return lax.ppermute(value, ("ctx", "head"), pairs)
    for c, step in ((0, 1), (1, -1)):
        for z in range(NZ):
            for y in range(NY):
                to_z = (z + step) % NZ if axis == "z" else z
                to_y = (y + step) % NY if axis == "y" else y
                pairs.append(((c * NZ + z) * NY + y, (c * NZ + to_z) * NY + to_y))
    return lax.ppermute(value, ("ctx", "doc"), pairs)


def swap(value):
    return lax.ppermute(value, "ctx", [(0, 1), (1, 0)])


def pack_kernel(away, pattern, q, k, v, packed, sem):
    c = lax.axis_index("ctx")
    head = 1 - c if away else c
    cols = pl.ds(pl.multiple_of(head * HEAD_SIZE, HEAD_SIZE), HEAD_SIZE)
    for g in range(GROUP):
        at = pl.multiple_of(head * GROUP * HEAD_SIZE + g * HEAD_SIZE, HEAD_SIZE)
        pltpu.make_async_copy(q.at[:, pl.ds(at, HEAD_SIZE)], packed.at[2 * SLOTS + g], sem).start()
    many = 0
    for b in range(QB):
        count = 0
        for s in range(PICKS):
            block = pattern[b, s]
            mine = block // NKB_DEV == c
            row = pl.multiple_of((block % NKB_DEV) * BLOCK_TOKENS, BLOCK_TOKENS)
            slot = b * CAP + count

            @pl.when(mine)
            def _(row=row, slot=slot):
                rows = pl.ds(row, BLOCK_TOKENS)
                pltpu.make_async_copy(k.at[rows, cols], packed.at[slot], sem).start()
                pltpu.make_async_copy(v.at[rows, cols], packed.at[SLOTS + slot], sem).start()

            count = count + mine.astype(jnp.int32)
        many = many + count

    queries = packed.at[pl.ds(2 * SLOTS, GROUP)]
    pltpu.make_async_copy(queries, queries, sem).wait()

    def settle(_, carry):
        pair = packed.at[pl.ds(0, 2)]
        pltpu.make_async_copy(pair, pair, sem).wait()
        return carry

    lax.fori_loop(0, many, settle, 0)


def pack(away, pattern, q, k, v):
    def body(*refs):
        pack_kernel(away, *refs)

    return pl.pallas_call(
        body,
        out_shape=jax.ShapeDtypeStruct((SENT, BLOCK_TOKENS, HEAD_SIZE), BF16),
        in_specs=[pl.BlockSpec(memory_space=pltpu.SMEM), ANY, ANY, ANY],
        out_specs=pl.BlockSpec(memory_space=pltpu.VMEM),
        scratch_shapes=[pltpu.SemaphoreType.DMA],
        name="pack_away" if away else "pack_here",
    )(pattern, q, k, v)


def attend_kernel(pattern, kept, got, out, turned, qs, ks, vs):
    c = lax.axis_index("ctx")
    for b in range(QB):
        count = 0
        for s in range(PICKS):
            count = count + (pattern[b, s] // NKB_DEV == c).astype(jnp.int32)
        for kind, chosen in enumerate((ks, vs)):
            slots = pl.ds(kind * SLOTS + b * CAP, CAP)
            chosen[b, pl.ds(0, CAP)] = kept[slots]
            chosen[b, pl.ds(count, CAP)] = got[slots]
        for source, here in ((kept, c == b), (got, c != b)):

            @pl.when(here)
            def _(source=source, b=b):
                qs[b] = source[pl.ds(2 * SLOTS, GROUP)]

    for b in range(QB):
        keys = ks[b, :PICKS].reshape(PICKS * BLOCK_TOKENS, HEAD_SIZE)
        vals = vs[b, :PICKS].reshape(PICKS * BLOCK_TOKENS, HEAD_SIZE)
        for pair in range(GROUP // 2):
            rows = qs[b, 2 * pair : 2 * pair + 2].reshape(2 * BLOCK_TOKENS, HEAD_SIZE)
            scores = lax.dot_general(rows, keys, (((1,), (1,)), ((), ())), preferred_element_type=F32)
            top = jnp.max(scores, axis=-1, keepdims=True)
            weights = jnp.exp2((scores - top) * SCALE)
            total = jnp.sum(weights, axis=-1, keepdims=True)
            mixed = jnp.dot(weights.astype(BF16), vals, preferred_element_type=F32) / total
            for i in range(2):
                g = 2 * pair + i
                part = mixed[i * BLOCK_TOKENS : (i + 1) * BLOCK_TOKENS]
                cols = pl.ds(g * HEAD_SIZE, HEAD_SIZE)
                out[jnp.where(c == b, 0, 1), :, cols] = part.astype(BF16)
                turned[cols, pl.ds(b * BLOCK_TOKENS, BLOCK_TOKENS)] = part.T.astype(BF16)


def attend(pattern, kept, got):
    width = GROUP * HEAD_SIZE
    out = jax.ShapeDtypeStruct((QB, BLOCK_TOKENS, width), BF16)
    chosen = pltpu.VMEM((QB, 2 * CAP, BLOCK_TOKENS, HEAD_SIZE), BF16)
    vmem = pl.BlockSpec(memory_space=pltpu.VMEM)
    return pl.pallas_call(
        attend_kernel,
        out_shape=(out, jax.ShapeDtypeStruct((width, QB * BLOCK_TOKENS), BF16)),
        in_specs=[pl.BlockSpec(memory_space=pltpu.SMEM), vmem, vmem],
        out_specs=(vmem, vmem),
        scratch_shapes=[
            pltpu.VMEM((QB, GROUP, BLOCK_TOKENS, HEAD_SIZE), BF16),
            chosen,
            chosen,
        ],
        compiler_params=pltpu.CompilerParams(vmem_limit_bytes=32 << 20),
        name="attend",
    )(pattern, kept, got)


def product_kernel(tasks, *refs):
    lefts = refs[:4], refs[4:8]
    rights = tuple(zip(refs[8:12], refs[12:16]))
    outs, bt = refs[16:-1], refs[-1]
    c, x = lax.axis_index("ctx"), lax.axis_index("head")
    z = lax.axis_index("doc") // NY
    for i in sorted({i for i, _ in tasks}):
        owner = lax.rem(z + jnp.where(c == 0, 4 - i, 4 + i), NZ)
        away = lax.rem(owner // 2 + NX - x, NX)
        other = (lax.rem(owner, 2) != c).astype(jnp.int32)
        side = jnp.where(c == 0, 3, 1)
        case = jnp.where(away == 0, 0, jnp.where(away == 2, 3, jnp.where(away == side, 1, 2)))
        for k in range(4):
            for r in range(2):

                @pl.when(jnp.logical_and(case == k, other == r))
                def _(k=k, r=r):
                    bt[...] = rights[k][r][...]

        for r in sorted({r for j, r in tasks if j == i}):
            total = None
            for left, doc in zip(lefts[r], (0, 1 + c, 2 - c, 3)):
                dims = (((1,), (1,)), ((), ()))
                term = lax.dot_general(left[...], bt[doc], dims, preferred_element_type=F32)
                total = term if total is None else total + term
            out = outs[tasks.index((i, r))]
            out[...] = total.astype(out.dtype)


def products(tasks, lefts, rights):
    rows, cols = GROUP * HEAD_SIZE, 2 * HEAD_SIZE
    vmem = pl.BlockSpec(memory_space=pltpu.VMEM)

    def body(*refs):
        product_kernel(tasks, *refs)

    return pl.pallas_call(
        body,
        out_shape=[jax.ShapeDtypeStruct((rows, cols), F32 if i == 4 else BF16) for i, _ in tasks],
        in_specs=[vmem] * 16,
        out_specs=[vmem] * len(tasks),
        scratch_shapes=[pltpu.VMEM((NY, cols, QB * BLOCK_TOKENS), BF16)],
        compiler_params=pltpu.CompilerParams(vmem_limit_bytes=16 << 20),
        name="products",
    )(*lefts[0], *lefts[1], *rights[0], *rights[1])


def added(got, here):
    return (got.astype(F32) + here.astype(F32)).astype(BF16)


def per_device(queries, keys, values, pattern):
    c = lax.axis_index("ctx")
    y = lax.axis_index("doc") % NY
    q, k, v, chosen = queries[0], keys[0], values[0], pattern[0]
    got = swap(pack(True, chosen, q, k, v))
    kept = pack(False, chosen, q, k, v)
    out, turned = attend(chosen, kept, got)
    cols = 2 * HEAD_SIZE

    def share(step):
        return lax.dynamic_slice_in_dim(turned, ((y + step) % NY) * cols, cols, 0)

    mine = jnp.stack([share(0), hop(share(1), 1), hop(share(-1), -1), hop(share(2), 2)])
    x1 = toward(mine, "x")
    whole, _ = lax.optimization_barrier((turned, mine))
    y1 = toward(whole, "y")
    mine_other, turned_other = swap(mine), swap(turned)
    x1_other, y1_other = toward(mine_other, "x"), toward(turned_other, "y")
    x2, y2 = toward(x1, "x"), toward(y1, "y")
    lefts = [turned, y1, swap(y1_other), y2], [turned_other, y1_other, swap(y1), swap(y2)]
    rights = [mine, x1, swap(x1_other), x2], [mine_other, x1_other, swap(x1), swap(x2)]

    [first] = products([(0, 0)], lefts, rights)
    second = products([(1, 0), (1, 1)], lefts, rights)
    third = products([(2, 0), (2, 1), (3, 0), (3, 1), (4, 0)], lefts, rights)
    long = toward(first, "z")
    short = toward(second[1], "z")
    long = toward(added(long, second[0]), "z")
    short = toward(added(short, third[1]), "z")
    long = toward(added(long, third[0]), "z")
    short = toward(added(short, third[3]), "z")
    long = toward(added(long, third[2]), "z")
    gram = third[4] + swap(short).astype(F32) + long.astype(F32)

    own, returned = out[0], swap(out[1])
    attended = jnp.where(
        c == 0,
        jnp.concatenate([own, returned], axis=1),
        jnp.concatenate([returned, own], axis=1),
    )
    return (attended[None], gram)


def solution(mesh):
    placed = (
        P("doc", "ctx", "head"),
        P("doc", "ctx", "head"),
        P("doc", "ctx", "head"),
        P("doc", None, None),
    )
    return jax.shard_map(
        per_device,
        mesh=mesh,
        in_specs=placed,
        out_specs=(P("doc", "ctx", "head"), P(("head", "ctx"), "doc")),
        check_vma=False,
    )
```
